32 devices in a mesh: grp: 2 (over y), ep: 4 (over z), tp: 2 (over x), pp: 2 (over core).
Axes of the slice: x: 2, y: 2, z: 4, core: 2. Of those that a mesh axis runs over, the one named last changes fastest.
Arguments:
- queries: bfloat16 [2048, 8192], P(('grp', 'ep', 'pp'), 'tp'), parts along dimension 0, may hold values from -64 to 64
- suffix_keys: bfloat16 [2048, 512], P(('grp', 'ep', 'pp')), parts along dimension 0, may hold values from -6 to 6
- suffix_values: bfloat16 [2048, 512], P(('grp', 'ep', 'pp')), parts along dimension 0, may hold values from -6 to 6
- prefix_keys: bfloat16 [4096, 512], P(('grp', 'ep', 'pp')), parts along dimension 0, may hold values from -8 to 8
- prefix_values: bfloat16 [4096, 512], P(('grp', 'ep', 'pp')), parts along dimension 0, may hold values from -6 to 6
- prefix_groups: int32 [4096], P(('grp', 'ep', 'pp')), parts along dimension 0, may hold values from 0 to 7, never falling along the last dimension, each value on 1 to 1024 neighbouring positions
- shot_counts: int32 [16], P(('grp', 'ep', 'pp')), parts along dimension 0, may hold values from 1 to 8
- lengths: int32 [16], P(('grp', 'ep', 'pp')), parts along dimension 0, may hold values from 32 to 128
- hidden: bfloat16 [2048, 4096], P(('grp', 'ep', 'pp')), parts along dimension 0, may hold values from -6 to 6
- expert_ids: int32 [2048, 8], P(('grp', 'ep')), parts along dimension 0, may hold values from 0 to 127, all different within a row
- gate_weights: float32 [2048, 8], P(('grp', 'ep')), parts along dimension 0, may hold values from 0.1 to 1
- gate_proj: bfloat16 [4, 4096, 1536], P('ep', 'pp', 'tp'), may hold values from -0.09375 to 0.09375
- up_proj: bfloat16 [4, 4096, 1536], P('ep', 'pp', 'tp'), may hold values from -0.09375 to 0.09375
- down_proj: bfloat16 [4, 1536, 4096], P('ep', 'tp', 'pp'), may hold values from -0.15625 to 0.15625
Outputs:
- context: bfloat16 [2048, 8192], P(('grp', 'ep', 'pp'), 'tp'), parts along dimension 0
- moe_out: bfloat16 [2048, 4096], P(('grp', 'ep'), ('pp', 'tp')), parts along dimension 0
The draws below stay inside these ranges and needn't reach their ends.
There are 2 independent parts, one for each index of `grp`. The reference program is written for one: setup_inputs(seed, part) draws one part's arguments, and reference() takes and returns one part's arrays. A program takes and returns all parts, laid end to end along the dimension named above; an argument that names none is the same for every part. Nothing has to cross between parts.
All inputs are finite; a program needn't handle non-finite values.
Results may differ from the reference program's by a relative error of at most 0.022.
Values may be sent and summed in bfloat16 or wider, within the bound.
No kernel may reach another device: no remote copies, remote signals or barrier semaphores. Data moves between devices by JAX's collectives and lax.ppermute only.
A program may use at most 128 MiB of HBM per device.

```python
import math
import jax
import jax.numpy as jnp
import numpy as np
from jax import lax

D = 4096
FF = 1536
HEADS = 64
KVH = 4
HD = 128
EXPERTS_ALL = 128
TOP = 8
PREFIX = 2048
SUFFIX = 128
SHOTS = 8
TOK_DEV = 128
SUFFIXES = 8
TOKENS = 1024
EXPERTS = 4
CAP = 12


def draw_queries(key, part):
    values = 1.5 * jax.random.truncated_normal(jax.random.fold_in(key, 11), -6.0, 6.0, (TOKENS, HEADS, HD), jnp.float32)
    return values.reshape(TOKENS, HEADS * HD).astype(jnp.bfloat16)


def draw_prefix_keys(key, part):
    values = jax.random.truncated_normal(jax.random.fold_in(key, 13), -4.0, 4.0, (PREFIX, KVH, HD), jnp.float32)
    return values.reshape(PREFIX, KVH * HD).astype(jnp.bfloat16)


def plant(values, key, least, high):
    place = [jax.random.randint(jax.random.fold_in(key, axis), (), 0, length) for axis, length in enumerate(values.shape)]
    longest = values.shape.index(max(values.shape))
    beside = place[:longest] + [(place[longest] + 1) % values.shape[longest]] + place[longest + 1:]
    return values.at[tuple(place)].set(least).at[tuple(beside)].set(high)


def block_levels(key, extent, split, smallest, top_value):
    factor_of, own = 1.0, jax.random.fold_in(key, 6)
    for dim, blocks in split:
        heights = jnp.exp(jax.random.uniform(jax.random.fold_in(own, dim), (blocks,), jnp.float32, smallest / len(split), top_value / len(split)))
        factor_of = factor_of * jnp.repeat(heights, extent[dim] // blocks).reshape([-1 if axis == dim else 1 for axis in range(len(extent))])
    return factor_of


def different_ones(own_key, rows, amount, top, lift):
    sequence = jax.random.permutation(jax.random.fold_in(own_key, 1), amount)
    pull = sequence
    for power in range(3):
        pull = pull * pull // amount
    pull = pull * lift // amount
    tickets = jax.random.randint(jax.random.fold_in(own_key, 2), (rows, amount), 0, 4096) + pull
    sure = jax.random.permutation(jax.random.fold_in(own_key, 3), rows)[jnp.arange(amount) % rows]
    tickets = jnp.where(jnp.arange(rows)[:, None] == sure[None, :], 1 << 14, tickets)
    score = tickets * amount + jnp.arange(amount)
    return lax.top_k(score.astype(jnp.int32), top)[1].astype(jnp.int32)


def length_profile(amount, total, bound, skew):
    weights = [(1 << 20) // math.isqrt(rank ** skew) + 1 for rank in range(2, amount + 1)]
    surplus, counts = total - bound - (amount - 1), [1] * (amount - 1)
    while surplus > 0:
        movable = [i for i in range(amount - 1) if counts[i] < bound]
        mass, remaining = sum([weights[i] for i in movable]), surplus
        for i in movable:
            addition = min(bound - counts[i], max(1, remaining * weights[i] // mass), surplus)
            counts[i] = counts[i] + addition
            surplus = surplus - addition
    return np.array([bound] + counts)


def uneven_parts(stream_key, amount, total, reach, skew):
    if amount == 2:
        one = jax.random.randint(stream_key, (), max(1, total - reach), min(reach, total - 1) + 1)
        return jnp.stack([one, total - one])
    sizes = jnp.asarray(length_profile(amount, total, reach, skew), jnp.int32)
    twos = (amount - 1) // 2
    source_of, receiver = sizes[1:1 + 2 * twos:2], sizes[2:2 + 2 * twos:2]
    room = jnp.minimum(source_of - 1, reach - receiver)
    moved = jax.random.randint(jax.random.fold_in(stream_key, 1), (twos,), 0, 1 << 20) % (room + 1)
    sizes = sizes.at[1:1 + 2 * twos:2].set(source_of - moved).at[2:2 + 2 * twos:2].set(receiver + moved)
    return sizes[jax.random.permutation(jax.random.fold_in(stream_key, 2), amount)]


def normal_values(key, extent, spread, bound, shards=(), kind=jnp.bfloat16):
    array = jax.random.normal(key, extent, jnp.float32) * spread
    if len(shards) > 0:
        array = block_levels(key, extent, shards, -0.22, 0.18) * array
    return jnp.clip(array, min=-bound, max=bound).astype(kind)


def setup_inputs(seed: int = 0, part: int = 0) -> dict:
    key_list = jax.random.split(jax.random.key(seed), 15)
    part_keys = jax.random.split(jax.random.fold_in(key_list[14], part), 15)
    return {
        "queries": draw_queries(jax.random.fold_in(jax.random.fold_in(key_list[14], part), 71), part),
        "suffix_keys": normal_values(part_keys[1], (TOKENS, KVH * HD), 1.0, 6.0, ((0, 8),)),
        "suffix_values": normal_values(part_keys[2], (TOKENS, KVH * HD), 1.0, 6.0, ((0, 8),)),
        "prefix_keys": draw_prefix_keys(jax.random.fold_in(jax.random.fold_in(key_list[14], part), 71), part),
        "prefix_values": normal_values(part_keys[4], (PREFIX, KVH * HD), 1.0, 6.0, ((0, 8),)),
        "prefix_groups": jnp.searchsorted(jnp.cumsum(uneven_parts(part_keys[5], SHOTS, PREFIX, PREFIX // 2, 1)), jnp.arange(PREFIX), side="right").astype(jnp.int32),
        "shot_counts": plant(jax.random.randint(part_keys[6], (SUFFIXES,), 1, SHOTS + 1), jax.random.fold_in(part_keys[6], 1), 1, SHOTS).astype(jnp.int32),
        "lengths": plant(jax.random.randint(part_keys[7], (SUFFIXES,), SUFFIX // 4, SUFFIX + 1), jax.random.fold_in(part_keys[7], 1), SUFFIX // 4, SUFFIX).astype(jnp.int32),
        "hidden": normal_values(part_keys[8], (TOKENS, D), 1.0, 6.0, ((0, 8),)),
        "expert_ids": different_ones(part_keys[9], TOKENS, EXPERTS_ALL, TOP, 512),
        "gate_weights": jnp.clip(jnp.exp(math.log(1.0) - 2.3025851 * jax.random.uniform(part_keys[10], (TOKENS, TOP), jnp.float32) ** block_levels(part_keys[10], (TOKENS, TOP), ((0, 4),), -0.2, 0.2)), 0.1, 1.0),
        "gate_proj": normal_values(key_list[11], (EXPERTS, D, FF), D ** -0.5, 0.09375, ((0, 4), (1, 2), (2, 2))),
        "up_proj": normal_values(key_list[12], (EXPERTS, D, FF), D ** -0.5, 0.09375, ((0, 4), (1, 2), (2, 2))),
        "down_proj": normal_values(key_list[13], (EXPERTS, FF, D), FF ** -0.5, 0.15625, ((0, 4), (1, 2), (2, 2))),
    }


NEG = -1.0e30


def attend(query_block, suffix_key_block, suffix_value_block, length, shot_count, prefix_keys, prefix_values, prefix_groups):
    head_group = HEADS // KVH
    query_heads = query_block.reshape(SUFFIX, KVH, head_group, HD).astype(jnp.float32)
    key_rows = jnp.concatenate([prefix_keys, suffix_key_block], axis=0).reshape(PREFIX + SUFFIX, KVH, HD).astype(jnp.float32)
    value_rows = jnp.concatenate([prefix_values, suffix_value_block], axis=0).reshape(PREFIX + SUFFIX, KVH, HD).astype(jnp.float32)
    scores = jnp.einsum("tkgd,skd->tkgs", query_heads, key_rows) * (HD ** -0.5)
    position = jnp.arange(SUFFIX, dtype=jnp.int32)
    prefix_seen = jnp.broadcast_to((prefix_groups < shot_count)[None, :], (SUFFIX, PREFIX))
    own_seen = (position[None, :] <= position[:, None]) & (position[None, :] < length)
    visible = jnp.concatenate([prefix_seen, own_seen], axis=1)[:, None, None, :]
    scores = jnp.where(visible, scores, NEG)
    row_max = jnp.max(scores, axis=-1, keepdims=True)
    weights = jnp.where(visible, jnp.exp(scores - row_max), 0.0)
    denominator = jnp.sum(weights, axis=-1)
    rounded = lax.optimization_barrier(weights.astype(jnp.bfloat16)).astype(jnp.float32)
    attended = jnp.einsum("tkgs,skd->tkgd", rounded, value_rows) / denominator[..., None]
    attended = jnp.where((position < length)[:, None, None, None], attended, 0.0)
    return attended.reshape(SUFFIX, HEADS * HD).astype(jnp.bfloat16)


def routing(expert_ids, gate_weights, blocks):
    routed = expert_ids.reshape(blocks, TOK_DEV, TOP)
    gate_share = gate_weights.reshape(blocks, TOK_DEV, TOP)
    matches = routed[..., None] == jnp.arange(EXPERTS, dtype=jnp.int32)
    taken = jnp.sum(matches.astype(jnp.int32), axis=2)
    shares = jnp.sum(jnp.where(matches, gate_share[..., None], 0.0), axis=2)
    slot_index = jnp.cumsum(taken, axis=1) - taken
    served = (taken > 0) & (slot_index < CAP)
    return slot_index, served, shares


def reference(queries, suffix_keys, suffix_values, prefix_keys, prefix_values, prefix_groups, shot_counts, lengths, hidden, expert_ids, gate_weights, gate_proj, up_proj, down_proj):
    def attend_items(items):
        return attend(items[0], items[1], items[2], items[3], items[4], prefix_keys, prefix_values, prefix_groups)

    context = lax.map(attend_items, (queries.reshape(SUFFIXES, SUFFIX, HEADS * HD), suffix_keys.reshape(SUFFIXES, SUFFIX, KVH * HD), suffix_values.reshape(SUFFIXES, SUFFIX, KVH * HD), lengths, shot_counts))
    context = context.reshape(TOKENS, HEADS * HD)

    blocks = TOKENS // TOK_DEV
    slot_index, served, shares = routing(expert_ids, gate_weights, blocks)
    source = jnp.arange(blocks, dtype=jnp.int32)[:, None, None]
    row_index = jnp.where(served, source * CAP + slot_index, blocks * CAP).astype(jnp.int32)
    token_index = jnp.broadcast_to(jnp.arange(TOKENS, dtype=jnp.int32).reshape(blocks, TOK_DEV, 1), row_index.shape)

    def one_expert(expert):
        target = jnp.take(row_index, expert, axis=2).reshape(-1)
        owners = jnp.take(token_index, expert, axis=2).reshape(-1)
        owner = jnp.zeros((blocks * CAP,), jnp.int32).at[target].set(owners, mode="drop")
        filled = jnp.zeros((blocks * CAP,), jnp.bool_).at[target].set(True, mode="drop")
        inputs = jnp.where(filled[:, None], hidden[owner], 0)
        gate = jnp.dot(inputs, gate_proj[expert], preferred_element_type=jnp.float32)
        upward = jnp.dot(inputs, up_proj[expert], preferred_element_type=jnp.float32)
        active = (jax.nn.silu(gate) * upward).astype(jnp.bfloat16)
        return jnp.dot(active, down_proj[expert], preferred_element_type=jnp.float32).astype(jnp.bfloat16)

    expert_out = lax.map(one_expert, jnp.arange(EXPERTS, dtype=jnp.int32))

    def add_expert(running, expert):
        picked = lax.dynamic_index_in_dim(expert_out, expert, 0, keepdims=False)
        gather_rows = jnp.minimum(jnp.take(row_index, expert, axis=2), blocks * CAP - 1).reshape(-1)
        coefficient = jnp.where(jnp.take(served, expert, axis=2), jnp.take(shares, expert, axis=2), 0.0).reshape(-1)
        return running + coefficient[:, None] * picked[gather_rows].astype(jnp.float32), None

    moe_sum, unused_rest = lax.scan(add_expert, jnp.zeros((TOKENS, D), jnp.float32), jnp.arange(EXPERTS, dtype=jnp.int32))
    return context, moe_sum.astype(jnp.bfloat16)
```

```python
import functools
import math

import jax
import jax.numpy as jnp
from jax import lax
from jax.experimental import pallas as pl
from jax.experimental.pallas import tpu as pltpu
from jax.sharding import PartitionSpec as P

D = 4096
HEADS = 64
KVH = 4
HD = 128
TOP = 8
SUFFIX = 128
CAP = 12

NEG = -1e30
SCORE_SCALE = HD ** (-0.5) * math.log2(math.e)
GROUP_ROWS = 16


BF = jnp.bfloat16
F32 = jnp.float32
VMEM = pl.BlockSpec(memory_space=pltpu.VMEM)
SMEM = pl.BlockSpec(memory_space=pltpu.SMEM)


def dot(a, b, dims=(((1,), (0,)), ((), ()))):
    return lax.dot_general(a, b, dims, preferred_element_type=F32)


def params(mib=40, **kw):
    return pltpu.CompilerParams(vmem_limit_bytes=mib << 20, **kw)


def cost(flops, nbytes):
    return pl.CostEstimate(flops=int(flops), bytes_accessed=int(nbytes), transcendentals=0)


def pack_kernel(width, head_block, k_ref, v_ref, g_ref, out_ref):
    rows = k_ref.shape[0]
    first = pl.multiple_of(head_block(lax.axis_index("tp")) * width, 128)
    out_ref[0:rows, :] = k_ref[:, pl.ds(first, width)]
    out_ref[rows : 2 * rows, :] = v_ref[:, pl.ds(first, width)]
    lines = g_ref.shape[0]
    groups = g_ref[...].astype(F32)
    pad = jnp.full((GROUP_ROWS - lines, groups.shape[1]), 0.0, F32)
    groups = jnp.concatenate([groups, pad], axis=0)
    if groups.shape[1] < width:
        filler = jnp.zeros((GROUP_ROWS, width - groups.shape[1]), F32)
        groups = jnp.concatenate([groups, filler], axis=1)
    out_ref[2 * rows :, :] = groups.astype(BF)


def make_pack(keys, values, groups, width, head_block):
    rows = keys.shape[0]
    lines = max(1, rows // width)
    return pl.pallas_call(
        functools.partial(pack_kernel, width, head_block),
        out_shape=jax.ShapeDtypeStruct((2 * rows + GROUP_ROWS, width), BF),
        in_specs=[VMEM] * 3,
        out_specs=VMEM,
        compiler_params=params(8),
        cost_estimate=cost(0, 4 * rows * width * 4),
        name="pack",
    )(keys, values, groups.reshape(lines, rows // lines))


def attend_kernel(cfg, shots_ref, len_ref, *refs):
    heads, per_kv, width, head_block, rows_of, first, last = cfg
    refs = list(refs)
    q_ref = refs.pop(0)
    if first:
        sk_ref, sv_ref = refs.pop(0), refs.pop(0)
    packs = [refs.pop(0) for _ in rows_of]
    if not first:
        acc_in, m_in, l_in = refs.pop(0), refs.pop(0), refs.pop(0)
    tok = q_ref.shape[0]
    kv = (pl.program_id(0) * heads) // per_kv
    col = pl.ds(pl.multiple_of(kv * HD, HD), HD)
    shots = shots_ref[0].astype(F32)
    blocks = []
    if first:
        start = pl.multiple_of(head_block(lax.axis_index("tp")) * width + kv * HD, HD)
        lane = lax.broadcasted_iota(jnp.int32, (tok, tok), 1)
        line = lax.broadcasted_iota(jnp.int32, (tok, tok), 0)
        seen = (lane <= line) & (lane < len_ref[0])
        bias = jnp.where(seen, 0.0, NEG).astype(F32)
        blocks.append((sk_ref[:, pl.ds(start, HD)], sv_ref[:, pl.ds(start, HD)], bias))
    for rows, ref in zip(rows_of, packs):
        lines = max(1, rows // width)
        groups = [ref[2 * rows + n : 2 * rows + n + 1, : rows // lines] for n in range(lines)]
        groups = groups[0] if lines == 1 else jnp.concatenate(groups, axis=1)
        bias = jnp.where(groups.astype(F32) < shots, 0.0, NEG).astype(F32)
        blocks.append((ref[0:rows, col], ref[rows : 2 * rows, col], bias))
    values = [jnp.concatenate([v, jnp.ones_like(v)], axis=1) for _, v, _ in blocks]
    for n in range(heads):
        at = slice(n * HD, (n + 1) * HD)
        q = q_ref[:, at]
        scores = [
            dot(q, k, (((1,), (1,)), ((), ()))) * SCORE_SCALE + bias for k, _, bias in blocks
        ]
        peak = None
        for s in scores:
            for j in range(0, s.shape[1], 128):
                part = s[:, j : j + 128]
                peak = part if peak is None else jnp.maximum(peak, part)
        peak = jnp.max(peak, axis=1, keepdims=True)
        if not first:
            before = m_in[:, at]
            peak = jnp.maximum(jnp.broadcast_to(peak, before.shape), before)
        update = None
        for s, v in zip(scores, values):
            bound = peak if first else jnp.broadcast_to(peak[:, :1], s.shape)
            weight = jnp.exp2(s - bound).astype(BF)
            term = dot(weight, v)
            update = term if update is None else update + term
        top, total = update[:, :HD], update[:, HD:]
        if not first:
            factor = jnp.exp2(before - peak)
            top = top + acc_in[:, at] * factor
            total = total + l_in[:, at] * factor
        if last:
            (ctx_ref,) = refs
            live = lax.broadcasted_iota(jnp.int32, (tok, HD), 0) < len_ref[0]
            ctx_ref[:, at] = jnp.where(live, top / total, 0.0).astype(BF)
        else:
            acc_out, m_out, l_out = refs
            acc_out[:, at] = top
            m_out[:, at] = jnp.broadcast_to(peak, (tok, HD))
            l_out[:, at] = total


def attend(queries, shots, lengths, own, packs, state, last, per_kv, width, head_block):
    tok, columns = queries.shape
    local_heads = columns // HD
    heads = min(4, per_kv)
    first = state is None
    rows_of = tuple((p.shape[0] - GROUP_ROWS) // 2 for p in packs)
    cfg = (heads, per_kv, width, head_block, rows_of, first, last)
    head_spec = pl.BlockSpec((tok, heads * HD), lambda i: (0, i))

    def whole(a):
        return pl.BlockSpec(a.shape, lambda i: (0, 0))

    operands = [shots, lengths, queries]
    specs = [SMEM, SMEM, head_spec]
    for a in (list(own) if first else []) + list(packs):
        operands.append(a)
        specs.append(whole(a))
    if not first:
        operands += list(state)
        specs += [head_spec] * 3
    if last:
        shapes = jax.ShapeDtypeStruct((tok, columns), BF)
        outs = head_spec
    else:
        shapes = [jax.ShapeDtypeStruct((tok, columns), F32)] * 3
        outs = [head_spec] * 3
    keys = sum(rows_of) + (tok if first else 0)
    return pl.pallas_call(
        functools.partial(attend_kernel, cfg),
        out_shape=shapes,
        grid=(local_heads // heads,),
        in_specs=specs,
        out_specs=outs,
        compiler_params=params(40, dimension_semantics=("arbitrary",)),
        cost_estimate=cost(8 * tok * local_heads * keys * HD, 4 * tok * columns),
        name="attend",
    )(*operands)


def strict_lower(tok):
    line = lax.broadcasted_iota(jnp.int32, (tok, tok), 0)
    lane = lax.broadcasted_iota(jnp.int32, (tok, tok), 1)
    return jnp.where(lane < line, 1.0, 0.0).astype(BF)


def routes(ids, expert_of, shape, weights=None):
    taken = jnp.zeros(shape, F32)
    share = jnp.zeros(shape, F32)
    for k in range(TOP):
        match = jnp.broadcast_to(ids[:, k : k + 1], shape) == expert_of
        taken = jnp.where(match, 1.0, taken)
        if weights is not None:
            share = share + jnp.where(match, jnp.broadcast_to(weights[:, k : k + 1], shape), 0.0)
    slot = dot(strict_lower(shape[0]), taken.astype(BF)).astype(jnp.int32)
    return taken, slot, share


def dispatch_kernel(experts, parts, ids_ref, hidden_ref, out_ref):
    tok, model = hidden_ref.shape
    lanes = experts * 2 * CAP
    half = model // parts // 2
    ids = ids_ref[pl.ds(pl.multiple_of(lax.axis_index("pp") * tok, tok), tok), :]
    lane = lax.broadcasted_iota(jnp.int32, (tok, lanes), 1)
    taken, slot, _ = routes(ids, lane // (2 * CAP), (tok, lanes))
    chosen = (taken > 0.0) & (slot == lane % CAP)
    pick = jnp.where(chosen, 1.0, 0.0).astype(BF)
    upper = lax.broadcasted_iota(jnp.int32, (lanes, half), 0) % (2 * CAP) < CAP
    tn = (((0,), (0,)), ((), ()))
    for p in range(parts):
        low = dot(pick, hidden_ref[:, 2 * p * half : (2 * p + 1) * half], tn)
        high = dot(pick, hidden_ref[:, (2 * p + 1) * half : (2 * p + 2) * half], tn)
        rows = jnp.where(upper, low, high).astype(BF)
        for e in range(experts):
            out_ref[e * parts + p] = rows[e * 2 * CAP : (e + 1) * 2 * CAP, :]


def dispatch(ids, hidden, experts, parts):
    tok, model = hidden.shape
    shape = (experts * parts, 2 * CAP, model // parts // 2)
    return pl.pallas_call(
        functools.partial(dispatch_kernel, experts, parts),
        out_shape=jax.ShapeDtypeStruct(shape, BF),
        in_specs=[VMEM] * 2,
        out_specs=VMEM,
        compiler_params=params(16),
        cost_estimate=cost(4 * tok * model * experts * CAP, 2 * tok * model),
        name="dispatch",
    )(ids, hidden)


def gateup_kernel(x_ref, gate_ref, up_ref, out_ref, sum_ref, rows_ref):
    step = pl.program_id(0)
    blocks, _, half = x_ref.shape
    rows = blocks * CAP
    units = gate_ref.shape[2]
    depth = gate_ref.shape[1]

    @pl.when(step == 0)
    def _():
        x = x_ref[...].reshape(blocks * 2 * CAP, half)
        line = lax.broadcasted_iota(jnp.int32, (rows, blocks * 2 * CAP), 0)
        lane = lax.broadcasted_iota(jnp.int32, (rows, blocks * 2 * CAP), 1)
        base = (line // CAP) * (2 * CAP) + line % CAP
        for h in range(2):
            pick = jnp.where(lane == base + h * CAP, 1.0, 0.0).astype(BF)
            picked = dot(pick, x).astype(BF)
            for n in range(half // depth):
                rows_ref[h * (half // depth) + n] = picked[:, n * depth : (n + 1) * depth]

    x = rows_ref[step]
    for n, w_ref in enumerate((gate_ref, up_ref)):
        at = slice(n * units, (n + 1) * units)
        part = dot(x, w_ref[0])

        @pl.when(step == 0)
        def _():
            sum_ref[:, at] = part

        @pl.when(step > 0)
        def _():
            sum_ref[:, at] += part

    @pl.when(step == pl.num_programs(0) - 1)
    def _():
        out_ref[...] = sum_ref[...].astype(BF)


def gateup(x, gate_proj, up_proj):
    blocks, _, half = x.shape
    _, model, units = gate_proj.shape
    rows = blocks * CAP
    depth = 512
    spec = pl.BlockSpec((1, depth, units), lambda i: (0, i, 0))
    return pl.pallas_call(
        gateup_kernel,
        out_shape=jax.ShapeDtypeStruct((rows, 2 * units), BF),
        grid=(model // depth,),
        in_specs=[pl.BlockSpec(x.shape, lambda i: (0, 0, 0)), spec, spec],
        out_specs=pl.BlockSpec((rows, 2 * units), lambda i: (0, 0)),
        scratch_shapes=[
            pltpu.VMEM((rows, 2 * units), F32),
            pltpu.VMEM((model // depth, rows, depth), BF),
        ],
        compiler_params=params(24, dimension_semantics=("arbitrary",)),
        cost_estimate=cost(4 * rows * model * units, 4 * model * units),
        name="gateup",
    )(x, gate_proj, up_proj)


def down_kernel(splits, mine_ref, other_ref, down_ref, *outs):
    units = mine_ref.shape[1] // 2
    total = mine_ref[...].astype(F32)
    for n in range(other_ref.shape[0]):
        total = total + other_ref[n].astype(F32)
    gate, up = total[:, :units], total[:, units:]
    active = (gate / (1.0 + jnp.exp(-gate)) * up).astype(BF)
    width = down_ref.shape[2] // splits
    me = lax.axis_index("tp")
    for n in range(splits):
        place = me ^ n if splits & (splits - 1) == 0 else lax.rem(me + n, splits)
        at = pl.ds(pl.multiple_of(place * width, 128), width)
        outs[n][...] = dot(active, down_ref[0, :, at]).astype(outs[n].dtype)


def down(mine, other, down_proj, splits):
    rows = mine.shape[0]
    _, units, model = down_proj.shape
    shapes = [jax.ShapeDtypeStruct((rows, model // splits), F32 if n == 0 else BF) for n in range(splits)]
    return pl.pallas_call(
        functools.partial(down_kernel, splits),
        out_shape=shapes,
        in_specs=[VMEM] * 3,
        out_specs=[VMEM] * splits,
        compiler_params=params(16),
        cost_estimate=cost(2 * rows * model * units, 2 * model * units),
        name="down",
    )(mine, other, down_proj)


def join_kernel(*refs):
    *parts, out_ref = refs
    total = parts[0][...]
    for p in parts[1:]:
        total = total + p[...].astype(F32)
    out_ref[...] = total.astype(BF).reshape(out_ref.shape)


def join(parts, experts):
    rows, width = parts[0].shape
    return pl.pallas_call(
        join_kernel,
        out_shape=jax.ShapeDtypeStruct((experts, rows // experts, width), BF),
        in_specs=[VMEM] * len(parts),
        out_specs=VMEM,
        compiler_params=params(8),
        cost_estimate=cost(rows * width, 8 * rows * width),
        name="join",
    )(*parts)


def combine_kernel(parts, ids_ref, weight_ref, back_ref, out_ref):
    experts, per, width = back_ref.shape
    lanes = experts * per
    tok = ids_ref.shape[0] // parts
    back = back_ref[...].reshape(lanes, width)
    lane = lax.broadcasted_iota(jnp.int32, (tok, lanes), 1)
    for p in range(parts):
        at = slice(p * tok, (p + 1) * tok)
        _, slot, share = routes(ids_ref[at, :], lane // per, (tok, lanes), weight_ref[at, :])
        place = lane % per
        chosen = (slot == place % CAP) & (place // CAP == p)
        table = jnp.where(chosen, share, 0.0)
        high = table.astype(BF)
        low = (table - high.astype(F32)).astype(BF)
        out_ref[at, :] = (dot(high, back) + dot(low, back)).astype(BF)


def combine(ids, weights, back, parts):
    tokens = ids.shape[0]
    return pl.pallas_call(
        functools.partial(combine_kernel, parts),
        out_shape=jax.ShapeDtypeStruct((tokens, back.shape[2]), BF),
        in_specs=[VMEM] * 3,
        out_specs=VMEM,
        compiler_params=params(16),
        cost_estimate=cost(4 * tokens * back.size // 2, 4 * back.size),
        name="combine",
    )(ids, weights, back)


def swaps(size, k):
    return [(i, i ^ k) for i in range(size)]


def others(a, axis, size):
    return [lax.ppermute(a, axis, [(i, (i + k) % size) for i in range(size)]) for k in range(1, size)]


def shards(
    queries,
    suffix_keys,
    suffix_values,
    prefix_keys,
    prefix_values,
    prefix_groups,
    shot_counts,
    lengths,
    hidden,
    expert_ids,
    gate_weights,
    gate_proj,
    up_proj,
    down_proj,
):
    ep, tp, pp = lax.axis_size("ep"), lax.axis_size("tp"), lax.axis_size("pp")
    local_heads = queries.shape[1] // HD
    head_group = HEADS // KVH
    kv_heads = max(1, local_heads // head_group)
    per_kv = min(local_heads, head_group)
    width = kv_heads * HD

    def head_block(tp_index):
        return (tp_index * local_heads // head_group) // kv_heads

    outgoing = dispatch(expert_ids, hidden, ep, pp)
    arrived = lax.all_to_all(outgoing, ("ep", "pp"), split_axis=0, concat_axis=0, tiled=True)

    pack = make_pack(prefix_keys, prefix_values, prefix_groups, width, head_block)
    rows = prefix_keys.shape[0]
    if ep & (ep - 1) == 0 and rows % 128 == 0:
        held = [pack]
        stride = ep // 2
        while stride:
            held += [lax.ppermute(b, "ep", swaps(ep, stride)) for b in held]
            stride //= 2
        packs = []
        for b in held:
            packs += [b] + others(b, "pp", pp)
    else:
        every = lax.all_gather(pack, ("ep", "pp"), axis=0)
        step = max(1, 256 // rows)
        keys = every[:, :rows].reshape(-1, step * rows, width)
        values = every[:, rows : 2 * rows].reshape(-1, step * rows, width)
        lines = max(1, rows // width)
        groups = every[:, 2 * rows : 2 * rows + lines, : rows // lines].reshape(-1, step * rows // width, width)
        groups = jnp.pad(groups, ((0, 0), (0, GROUP_ROWS - groups.shape[1]), (0, 0)))
        joined = jnp.concatenate([keys, values, groups], axis=1)
        packs = [joined[n] for n in range(joined.shape[0])]

    fixed = dict(per_kv=per_kv, width=width, head_block=head_block)
    own = (suffix_keys, suffix_values)
    context = attend(queries, shot_counts, lengths, own, packs, None, True, **fixed)

    mine = gateup(arrived, gate_proj, up_proj)
    other = jnp.stack(others(mine, "pp", pp)) if pp > 2 else others(mine, "pp", pp)[0][None]
    parts = down(mine, other, down_proj, tp)
    received = []
    for n in range(1, tp):
        if tp & (tp - 1) == 0:
            pairs = swaps(tp, n)
        else:
            pairs = [(i, (i + n) % tp) for i in range(tp)]
        received.append(lax.ppermute(parts[n], "tp", pairs))
    expert_out = join([parts[0]] + received, ep)
    back = lax.all_to_all(expert_out, "ep", split_axis=0, concat_axis=0, tiled=True)
    moe_out = combine(expert_ids, gate_weights, back, pp)
    return (context, moe_out)


def solution(mesh):
    placed = (
        P(("grp", "ep", "pp"), "tp"),
        P(("grp", "ep", "pp"), None),
        P(("grp", "ep", "pp"), None),
        P(("grp", "ep", "pp"), None),
        P(("grp", "ep", "pp"), None),
        P(("grp", "ep", "pp")),
        P(("grp", "ep", "pp")),
        P(("grp", "ep", "pp")),
        P(("grp", "ep", "pp"), None),
        P(("grp", "ep"), None),
        P(("grp", "ep"), None),
        P("ep", "pp", "tp"),
        P("ep", "pp", "tp"),
        P("ep", "tp", "pp"),
    )
    return jax.shard_map(
        shards,
        mesh=mesh,
        in_specs=placed,
        out_specs=(P(("grp", "ep", "pp"), "tp"), P(("grp", "ep"), ("pp", "tp"))),
        check_vma=False,
    )
```

```python
import functools
import math

import jax
import jax.numpy as jnp
from jax import lax
from jax.experimental import pallas as pl
from jax.experimental.pallas import tpu as pltpu
from jax.sharding import PartitionSpec as P


HEADS = 64
KVH = 4
HD = 128
TOP = 8
CAP = 12

NEG = -1e30
SCORE_SCALE = HD ** (-0.5) * math.log2(math.e)
GROUP_ROWS = 16
STACK = 2
ATT_MIB = 24
VMEM_ALL = 67043328
SELECT_KIB = 960


BF = jnp.bfloat16
F32 = jnp.float32
VMEM = pl.BlockSpec(memory_space=pltpu.VMEM)
ANY = pl.BlockSpec(memory_space=pl.ANY)
HBM = pl.BlockSpec(memory_space=pltpu.HBM)


def dot(a, b, dims=(((1,), (0,)), ((), ()))):
    return lax.dot_general(a, b, dims, preferred_element_type=F32)


def params(mib=40, **kw):
    return pltpu.CompilerParams(vmem_limit_bytes=mib << 20, **kw)


def cost(flops, nbytes):
    return pl.CostEstimate(flops=int(flops), bytes_accessed=int(nbytes), transcendentals=0)


def attend_kernel(cfg, facts_ref, *refs):
    per_kv, width, head_block, rows_of, first, previous, last, waits = cfg
    refs = list(refs)
    q_ref = refs.pop(0)
    if first:
        sk_ref, sv_ref = refs.pop(0), refs.pop(0)
    packs = [refs.pop(0) for _ in rows_of]
    before = [(refs.pop(0), refs.pop(0)) for _ in range(previous)]
    del refs[:waits]
    tok, columns = q_ref.shape
    local_heads = columns // HD
    stack = min(STACK, per_kv)
    shots = facts_ref[0:1, 0:1]
    length = jnp.broadcast_to(facts_ref[8:9, :], (tok, 128))
    lane = lax.broadcasted_iota(jnp.int32, (tok, 128), 1)
    live = lax.broadcasted_iota(jnp.int32, (tok, HD), 0).astype(F32) < length
    if last:
        (ctx_ref,) = refs
    else:
        ctx_ref, lse_ref = refs
        lse_ref[...] = jnp.zeros((tok, 128), F32)
    for kv in range(local_heads // per_kv):
        col = slice(kv * HD, (kv + 1) * HD)
        blocks = []
        if first:
            start = pl.multiple_of(head_block(lax.axis_index("tp")) * width + kv * HD, HD)
            across = lax.broadcasted_iota(jnp.int32, (tok, tok), 1)
            line = lax.broadcasted_iota(jnp.int32, (tok, tok), 0)
            seen = (across <= line) & (across.astype(F32) < length)
            bias = jnp.where(seen, 0.0, NEG).astype(F32)
            bias = jnp.concatenate([bias] * stack, axis=0)
            blocks.append((sk_ref[:, pl.ds(start, HD)], sv_ref[:, pl.ds(start, HD)], bias))
        for rows, ref in zip(rows_of, packs):
            lines = max(1, rows // width)
            groups = [ref[2 * rows + n : 2 * rows + n + 1, : rows // lines] for n in range(lines)]
            groups = groups[0] if lines == 1 else jnp.concatenate(groups, axis=1)
            groups = groups.astype(F32)
            bias = jnp.where(groups < jnp.broadcast_to(shots, groups.shape), 0.0, NEG).astype(F32)
            blocks.append((ref[0:rows, col], ref[rows : 2 * rows, col], bias))
        blocks = [(k, jnp.concatenate([v, jnp.ones_like(v)], axis=1), b) for k, v, b in blocks]

        def group(base):
            ats = [slice((base + i) * HD, (base + i + 1) * HD) for i in range(stack)]
            q = jnp.concatenate([q_ref[:, at] for at in ats], axis=0)
            scores = [
                dot(q, k, (((1,), (1,)), ((), ()))) * SCORE_SCALE + bias for k, _, bias in blocks
            ]
            peak = None
            for s in scores:
                for j in range(0, s.shape[1], 128):
                    part = s[:, j : j + 128]
                    peak = part if peak is None else jnp.maximum(peak, part)
            peak = jnp.max(peak, axis=1, keepdims=True)
            update = None
            for s, (_, v, _) in zip(scores, blocks):
                term = dot(jnp.exp2(s - peak).astype(BF), v)
                update = term if update is None else update + term
            for i, at in enumerate(ats):
                r = slice(i * tok, (i + 1) * tok)
                top, total = update[r, :HD], update[r, HD:]
                mine = jnp.broadcast_to(peak[r], (tok, HD))
                if not last:
                    ctx_ref[:, at] = (top / total).astype(BF)
                    level = mine + jnp.log2(total)
                    lse_ref[...] = jnp.where(lane == base + i, level, lse_ref[...])
                    continue
                bound, levels = mine, []
                for _, lse in before:
                    level = jnp.broadcast_to(lse[:, base + i : base + i + 1], (tok, HD))
                    levels.append(level)
                    bound = jnp.maximum(bound, level)
                if before:
                    factor = jnp.exp2(mine - bound)
                    top, total = top * factor, total * factor
                for (ctx, _), level in zip(before, levels):
                    factor = jnp.exp2(level - bound)
                    top = top + ctx[:, at].astype(F32) * factor
                    total = total + factor
                ctx_ref[:, at] = jnp.where(live, top / total, 0.0).astype(BF)

        for i in range(0, per_kv, stack):
            group(kv * per_kv + i)


def attend(queries, facts, own, packs, before, last, per_kv, width, head_block, waits=()):
    tok, columns = queries.shape
    local_heads = columns // HD
    first = own is not None
    rows_of = tuple((p.shape[0] - GROUP_ROWS) // 2 for p in packs)
    cfg = (per_kv, width, head_block, rows_of, first, len(before), last, len(waits))
    operands = [facts, queries] + (list(own) if first else []) + list(packs)
    for pair in before:
        operands += list(pair)
    context = jax.ShapeDtypeStruct((tok, columns), BF)
    level = jax.ShapeDtypeStruct((tok, 128), F32)
    keys = sum(rows_of) + (tok if first else 0)
    return pl.pallas_call(
        functools.partial(attend_kernel, cfg),
        out_shape=context if last else [context, level],
        in_specs=[VMEM] * len(operands) + [ANY] * len(waits),
        out_specs=VMEM if last else [VMEM, VMEM],
        compiler_params=params(ATT_MIB),
        cost_estimate=cost(8 * tok * local_heads * keys * HD, 4 * tok * columns),
        name="attend",
    )(*operands, *waits)


def earlier(tok):
    line = lax.broadcasted_iota(jnp.int32, (tok, tok), 0)
    lane = lax.broadcasted_iota(jnp.int32, (tok, tok), 1)
    return jnp.where(line < lane, 1.0, 0.0).astype(BF)


def routes(ids, expert_of, weights=None):
    shape = expert_of.shape
    taken = jnp.zeros(shape, F32)
    share = jnp.zeros(shape, F32)
    for k in range(TOP):
        match = jnp.broadcast_to(ids[k : k + 1, :], shape) == expert_of
        taken = jnp.where(match, 1.0, taken)
        if weights is not None:
            share = share + jnp.where(match, jnp.broadcast_to(weights[k : k + 1, :], shape), 0.0)
    slot = dot(taken.astype(BF), earlier(shape[1])).astype(jnp.int32)
    return taken, slot, share


def pack_kernel(width, head_block, k_ref, v_ref, g_ref, shots_ref, len_ref, out_ref, facts_ref, *scratch):
    groups_ref, held_ref, line_ref, one_ref, two_ref, sem = scratch
    rows = k_ref.shape[0]
    first = pl.multiple_of(head_block(lax.axis_index("tp")) * width, 128)
    copies = [pltpu.make_async_copy(g_ref, groups_ref, sem.at[2])]
    for n, ref in enumerate((k_ref, v_ref)):
        place = held_ref.at[n * rows : (n + 1) * rows, :]
        copies.append(pltpu.make_async_copy(ref.at[:, pl.ds(first, width)], place, sem.at[n]))
    copies.append(pltpu.make_async_copy(shots_ref, one_ref, sem.at[4]))
    copies.append(pltpu.make_async_copy(len_ref, two_ref, sem.at[5]))
    for copy in copies:
        copy.start()
    copies[3].wait()
    copies[4].wait()
    line_ref[0:8, :] = jnp.full((8, 128), one_ref[0].astype(F32))
    line_ref[8:16, :] = jnp.full((8, 128), two_ref[0].astype(F32))
    facts = pltpu.make_async_copy(line_ref, facts_ref, sem.at[4])
    facts.start()
    copies[0].wait()
    groups = groups_ref[...].astype(F32)
    pad = jnp.full((GROUP_ROWS - groups.shape[0], groups.shape[1]), 0.0, F32)
    groups = jnp.concatenate([groups, pad], axis=0)
    if groups.shape[1] < width:
        filler = jnp.zeros((GROUP_ROWS, width - groups.shape[1]), F32)
        groups = jnp.concatenate([groups, filler], axis=1)
    held_ref[2 * rows :, :] = groups.astype(BF)
    copies[1].wait()
    copies[2].wait()
    store = pltpu.make_async_copy(held_ref, out_ref, sem.at[3])
    store.start()
    facts.wait()
    store.wait()


def make_pack(keys, values, groups, shots, lengths, width, head_block):
    rows = keys.shape[0]
    lines = max(1, rows // width)
    shape = (2 * rows + GROUP_ROWS, width)
    return pl.pallas_call(
        functools.partial(pack_kernel, width, head_block),
        out_shape=[jax.ShapeDtypeStruct(shape, BF), jax.ShapeDtypeStruct((16, 128), F32)],
        in_specs=[HBM] * 5,
        out_specs=[HBM] * 2,
        scratch_shapes=[
            pltpu.VMEM((lines, rows // lines), jnp.int32),
            pltpu.VMEM(shape, BF),
            pltpu.VMEM((16, 128), F32),
            pltpu.SMEM((1,), jnp.int32),
            pltpu.SMEM((1,), jnp.int32),
            pltpu.SemaphoreType.DMA((6,)),
        ],
        compiler_params=pltpu.CompilerParams(vmem_limit_bytes=VMEM_ALL),
        cost_estimate=cost(0, 4 * rows * width * 4),
        name="pack",
    )(keys, values, groups.reshape(lines, rows // lines), shots, lengths)


def target(me, n, size):
    return me ^ n if size & (size - 1) == 0 else lax.rem(me + n, size)


def select_kernel(cfg, place_ref, ids_ref, *refs):
    experts, parts = cfg
    hidden, outs = refs[:parts], refs[parts : parts + experts]
    own_ref, held_ref, here_ref, sem = refs[parts + experts :]
    tok, model = hidden[0].shape
    half = model // parts
    me = lax.axis_index("pp")
    column = pl.multiple_of(me * half, 128)
    copies = [pltpu.make_async_copy(ids_ref, own_ref, sem.at[0])]
    copies.append(pltpu.make_async_copy(place_ref, here_ref, sem.at[1 + parts]))
    for n in range(parts):
        source = hidden[n].at[:, pl.ds(column, half)]
        rows = held_ref.at[n * tok : (n + 1) * tok, :]
        copies.append(pltpu.make_async_copy(source, rows, sem.at[1 + n]))
    for copy in copies:
        copy.start()
    copies[0].wait()
    copies[1].wait()
    per = parts * CAP
    lines = experts * per
    row = lax.broadcasted_iota(jnp.int32, (lines, tok), 0)
    expert = target(here_ref[0], row // per, experts)
    picks = []
    for n in range(parts):
        block = lax.rem(me + parts - n, parts)
        ids = own_ref[:, pl.ds(pl.multiple_of(block * tok, tok), tok)]
        taken, slot, _ = routes(ids, expert)
        place = row % per
        chosen = (taken > 0.0) & (slot == place % CAP) & (place // CAP == block)
        picks.append(jnp.where(chosen, 1.0, 0.0))
    pick = jnp.concatenate(picks, axis=1)
    for copy in copies[2:]:
        copy.wait()
    for e in range(experts):
        outs[e][...] = dot(pick[e * per : (e + 1) * per, :].astype(BF), held_ref[...]).astype(BF)


def select(place, ids, hidden, experts, parts):
    tok, model = hidden[0].shape
    half = model // parts
    return pl.pallas_call(
        functools.partial(select_kernel, (experts, parts)),
        out_shape=[jax.ShapeDtypeStruct((parts * CAP, half), BF)] * experts,
        in_specs=[HBM] * (2 + parts),
        out_specs=[VMEM] * experts,
        scratch_shapes=[
            pltpu.VMEM(ids.shape, jnp.int32),
            pltpu.VMEM((parts * tok, half), BF),
            pltpu.SMEM((1,), jnp.int32),
            pltpu.SemaphoreType.DMA((2 + parts,)),
        ],
        compiler_params=pltpu.CompilerParams(vmem_limit_bytes=VMEM_ALL - (SELECT_KIB << 10)),
        cost_estimate=cost(4 * tok * model * experts * CAP, 2 * tok * model),
        name="select",
    )(place, ids, *hidden)


def mark_kernel(wait_ref, out_ref):
    out_ref[...] = jnp.zeros_like(out_ref)


def mark(wait, flops):
    return pl.pallas_call(
        mark_kernel,
        out_shape=jax.ShapeDtypeStruct((8, 128), F32),
        in_specs=[ANY],
        out_specs=VMEM,
        compiler_params=params(1),
        cost_estimate=cost(flops, 4096),
        name="mark",
    )(wait)


def gateup_kernel(pieces, waits, gate_ref, up_ref, *refs):
    out_ref = refs[pieces + waits]
    units = gate_ref.shape[2]
    x = jnp.concatenate([r[...].astype(F32) for r in refs[:pieces]], axis=0).astype(BF)
    for n, w_ref in enumerate((gate_ref, up_ref)):
        out_ref[:, n * units : (n + 1) * units] = dot(x, w_ref[0]).astype(BF)


def gateup(pieces, gate_proj, up_proj, waits=()):
    _, model, units = gate_proj.shape
    rows = sum(p.shape[0] for p in pieces)
    return pl.pallas_call(
        functools.partial(gateup_kernel, len(pieces), len(waits)),
        out_shape=jax.ShapeDtypeStruct((rows, 2 * units), BF),
        in_specs=[VMEM] * (2 + len(pieces)) + [ANY] * len(waits),
        out_specs=VMEM,
        compiler_params=params(16),
        cost_estimate=cost(4 * rows * model * units, 4 * model * units),
        name="gateup",
    )(gate_proj, up_proj, *pieces, *waits)


def down_kernel(splits, waits, mine_ref, other_ref, down_ref, *outs):
    outs = outs[waits:]
    units = mine_ref.shape[1] // 2
    total = mine_ref[...].astype(F32)
    for n in range(other_ref.shape[0]):
        total = total + other_ref[n].astype(F32)
    gate, up = total[:, :units], total[:, units:]
    active = (gate / (1.0 + jnp.exp(-gate)) * up).astype(BF)
    width = down_ref.shape[2] // splits
    me = lax.axis_index("tp")
    for n in range(splits):
        at = pl.ds(pl.multiple_of(target(me, n, splits) * width, 128), width)
        outs[n][...] = dot(active, down_ref[0, :, at]).astype(outs[n].dtype)


def down(mine, other, down_proj, splits, waits=()):
    rows = mine.shape[0]
    _, units, model = down_proj.shape
    shapes = [jax.ShapeDtypeStruct((rows, model // splits), F32 if n == 0 else BF) for n in range(splits)]
    return pl.pallas_call(
        functools.partial(down_kernel, splits, len(waits)),
        out_shape=shapes,
        in_specs=[VMEM] * 3 + [ANY] * len(waits),
        out_specs=[VMEM] * splits,
        compiler_params=params(16),
        cost_estimate=cost(2 * rows * model * units, 2 * model * units),
        name="down",
    )(mine, other, down_proj, *waits)


def join_kernel(experts, count, waits, *refs):
    parts, outs = refs[:count], refs[count + waits :]
    per = parts[0].shape[0] // experts
    for n in range(experts):
        at = slice(n * per, (n + 1) * per)
        total = parts[0][at, :]
        for p in parts[1:]:
            total = total + p[at, :].astype(F32)
        outs[n][...] = total.astype(BF)


def join(parts, experts, waits=()):
    rows, width = parts[0].shape
    return pl.pallas_call(
        functools.partial(join_kernel, experts, len(parts), len(waits)),
        out_shape=[jax.ShapeDtypeStruct((rows // experts, width), BF)] * experts,
        in_specs=[VMEM] * len(parts) + [ANY] * len(waits),
        out_specs=[VMEM] * experts,
        compiler_params=params(8),
        cost_estimate=cost(rows * width, 8 * rows * width),
        name="join",
    )(*parts, *waits)


def table_kernel(experts, parts, waits, place_ref, ids_ref, weight_ref, *refs):
    high_ref, low_ref, here_ref, sem = refs[waits:]
    copy = pltpu.make_async_copy(place_ref, here_ref, sem)
    copy.start()
    copy.wait()
    per = parts * CAP
    tok = ids_ref.shape[1] // parts
    row = lax.broadcasted_iota(jnp.int32, (experts * per, tok), 0)
    expert = target(here_ref[0], row // per, experts)
    place = row % per
    for p in range(parts):
        at = slice(p * tok, (p + 1) * tok)
        _, slot, share = routes(ids_ref[:, at], expert, weight_ref[:, at])
        chosen = (slot == place % CAP) & (place // CAP == p)
        table = jnp.where(chosen, share, 0.0)
        high = table.astype(BF)
        high_ref[:, at] = high
        low_ref[:, at] = (table - high.astype(F32)).astype(BF)


def make_table(place, ids, weights, experts, parts, waits=()):
    shape = jax.ShapeDtypeStruct((experts * parts * CAP, ids.shape[1]), BF)
    return pl.pallas_call(
        functools.partial(table_kernel, experts, parts, len(waits)),
        out_shape=[shape] * 2,
        in_specs=[HBM] + [VMEM] * 2 + [ANY] * len(waits),
        out_specs=[VMEM] * 2,
        scratch_shapes=[pltpu.SMEM((1,), jnp.int32), pltpu.SemaphoreType.DMA],
        compiler_params=params(8),
        cost_estimate=cost(1e6, 1e6),
        name="table",
    )(place, ids, weights, *waits)


def combine_kernel(high_ref, low_ref, *refs):
    backs, out_ref = refs[:-1], refs[-1]
    back = jnp.concatenate([b[...].astype(F32) for b in backs], axis=0).astype(BF)
    tn = (((0,), (0,)), ((), ()))
    out_ref[...] = (dot(high_ref[...], back, tn) + dot(low_ref[...], back, tn)).astype(BF)


def combine(high, low, backs):
    tokens = high.shape[1]
    width = backs[0].shape[1]
    return pl.pallas_call(
        combine_kernel,
        out_shape=jax.ShapeDtypeStruct((tokens, width), BF),
        in_specs=[VMEM] * (2 + len(backs)),
        out_specs=VMEM,
        compiler_params=params(16),
        cost_estimate=cost(4 * high.size * width, 4 * high.size + 2 * tokens * width),
        name="combine",
    )(high, low, *backs)


def swaps(size, k):
    return [(i, i ^ k) for i in range(size)]


def sends(size, n):
    if size & (size - 1) == 0:
        return swaps(size, n)
    return [(i, (i + n) % size) for i in range(size)]


def others(a, axis, size):
    return [lax.ppermute(a, axis, [(i, (i + k) % size) for i in range(size)]) for k in range(1, size)]


def layer(
    queries,
    suffix_keys,
    suffix_values,
    prefix_keys,
    prefix_values,
    prefix_groups,
    shot_counts,
    lengths,
    hidden,
    expert_ids,
    gate_weights,
    gate_proj,
    up_proj,
    down_proj,
):
    ep, tp, pp = lax.axis_size("ep"), lax.axis_size("tp"), lax.axis_size("pp")
    local_heads = queries.shape[1] // HD
    head_group = HEADS // KVH
    kv_heads = max(1, local_heads // head_group)
    per_kv = min(local_heads, head_group)
    width = kv_heads * HD

    def head_block(tp_index):
        return (tp_index * local_heads // head_group) // kv_heads

    rows = prefix_keys.shape[0]
    ids, shares = expert_ids.T, gate_weights.T
    place = lax.axis_index("ep").reshape(1)
    fixed = dict(per_kv=per_kv, width=width, head_block=head_block)
    own = (suffix_keys, suffix_values)

    features = [hidden] + others(hidden, "pp", pp)
    pack, facts = make_pack(
        prefix_keys, prefix_values, prefix_groups, shot_counts, lengths, width, head_block
    )
    basic = (queries, facts)
    outgoing = select(place, ids, features, ep, pp)
    started = mark(outgoing[0], 1e10)
    arrived = [outgoing[0]]
    for n in reversed(range(1, ep)):
        arrived.insert(1, lax.ppermute(outgoing[n], "ep", sends(ep, n)))

    ringed = ep & (ep - 1) == 0 and rows % 128 == 0
    if ringed:
        held = [pack]
        stride = ep // 2
        while stride:
            first, *rest = held
            moved = [lax.ppermute(first, "ep", swaps(ep, stride))]
            moved += [lax.ppermute(b, "ep", swaps(ep, stride)) for b in rest]
            held += moved
            stride //= 2
        order = [0, ep // 2] + [n for n in range(1, ep) if n != ep // 2]
        chips = [[held[n]] + others(held[n], "pp", pp) for n in order[:ep]]
    else:
        every = lax.all_gather(pack, ("ep", "pp"), axis=0)
        step = max(1, 256 // rows)
        keys = every[:, :rows].reshape(-1, step * rows, width)
        values = every[:, rows : 2 * rows].reshape(-1, step * rows, width)
        lines = max(1, rows // width)
        groups = every[:, 2 * rows : 2 * rows + lines, : rows // lines].reshape(-1, step * rows // width, width)
        groups = jnp.pad(groups, ((0, 0), (0, GROUP_ROWS - groups.shape[1]), (0, 0)))
        joined = jnp.concatenate([keys, values, groups], axis=1)
        chips = [[joined[n] for n in range(joined.shape[0])]]

    partial = []

    def attend_chip(n, waits):
        last = n == len(chips) - 1
        result = attend(
            *basic, own if n == 0 else None, chips[n], partial if last else [], last, waits=waits, **fixed
        )
        if not last:
            partial.append(result)
        return (result if last else result[1],)

    turn = iter(range(len(chips)))
    wait = attend_chip(next(turn), (started,)) if len(chips) > 1 else (started,)

    mine = gateup(arrived, gate_proj, up_proj, wait)
    other = others(mine, "pp", pp)
    other = jnp.stack(other) if pp > 2 else other[0][None]
    wait = attend_chip(next(turn), (mine,)) if len(chips) > 2 else (mine,)
    parts = down(mine, other, down_proj, tp, wait)
    high, low = make_table(place, ids, shares, ep, pp, (parts[0],))
    received = []
    for n in range(1, tp):
        received.append(lax.ppermute(parts[n], "tp", sends(tp, n)))
    wait = attend_chip(next(turn), (high,)) if len(chips) > 3 else ()
    done = join([parts[0]] + received, ep, wait)
    backs = [done[0]]
    for n in reversed(range(1, ep)):
        backs.insert(1, lax.ppermute(done[n], "ep", [(t, f) for f, t in sends(ep, n)]))
    returned = mark(done[0], 1e6)
    for n in turn:
        (context,) = attend_chip(n, (returned,))
    moe_out = combine(high, low, backs)
    return (context, moe_out)


def solution(mesh):
    placed = (
        P(("grp", "ep", "pp"), "tp"),
        P(("grp", "ep", "pp"), None),
        P(("grp", "ep", "pp"), None),
        P(("grp", "ep", "pp"), None),
        P(("grp", "ep", "pp"), None),
        P(("grp", "ep", "pp")),
        P(("grp", "ep", "pp")),
        P(("grp", "ep", "pp")),
        P(("grp", "ep", "pp"), None),
        P(("grp", "ep"), None),
        P(("grp", "ep"), None),
        P("ep", "pp", "tp"),
        P("ep", "pp", "tp"),
        P("ep", "tp", "pp"),
    )
    return jax.shard_map(
        layer,
        mesh=mesh,
        in_specs=placed,
        out_specs=(P(("grp", "ep", "pp"), "tp"), P(("grp", "ep"), ("pp", "tp"))),
        check_vma=False,
    )
```

```python
import functools
import math

import jax
import jax.numpy as jnp
from jax import lax
from jax.experimental import pallas as pl
from jax.experimental.pallas import tpu as pltpu
from jax.sharding import PartitionSpec as P


HEADS = 64
KVH = 4
HD = 128
TOP = 8
CAP = 12

NEG = -1e30
SCORE_SCALE = HD ** (-0.5) * math.log2(math.e)
GROUP_ROWS = 16
STACK = 2
ATT_MIB = 24
VMEM_ALL = 67043328


BF = jnp.bfloat16
F32 = jnp.float32
VMEM = pl.BlockSpec(memory_space=pltpu.VMEM)
ANY = pl.BlockSpec(memory_space=pl.ANY)
HBM = pl.BlockSpec(memory_space=pltpu.HBM)


def dot(a, b, dims=(((1,), (0,)), ((), ()))):
    return lax.dot_general(a, b, dims, preferred_element_type=F32)


def params(mib=40, **kw):
    return pltpu.CompilerParams(vmem_limit_bytes=mib << 20, **kw)


def cost(flops, nbytes):
    return pl.CostEstimate(flops=int(flops), bytes_accessed=int(nbytes), transcendentals=0)


def attend_kernel(cfg, facts_ref, *refs):
    per_kv, width, head_block, rows_of, first, previous, last, waits = cfg
    refs = list(refs)
    q_ref = refs.pop(0)
    if first:
        sk_ref, sv_ref = refs.pop(0), refs.pop(0)
    packs = [refs.pop(0) for _ in rows_of]
    before = [(refs.pop(0), refs.pop(0)) for _ in range(previous)]
    del refs[:waits]
    tok, columns = q_ref.shape
    local_heads = columns // HD
    stack = min(STACK, per_kv)
    shots = facts_ref[0:1, 0:1]
    length = jnp.broadcast_to(facts_ref[8:9, :], (tok, 128))
    lane = lax.broadcasted_iota(jnp.int32, (tok, 128), 1)
    live = lax.broadcasted_iota(jnp.int32, (tok, HD), 0).astype(F32) < length
    if last:
        out_ref, ctx_ref, lse_ref, store_ref, sem = refs
    else:
        ctx_ref, lse_ref = refs
    lse_ref[...] = jnp.zeros((tok, 128), F32)
    stores = []
    for kv in range(local_heads // per_kv):
        col = slice(kv * HD, (kv + 1) * HD)
        blocks = []
        if first:
            start = pl.multiple_of(head_block(lax.axis_index("tp")) * width + kv * HD, HD)
            across = lax.broadcasted_iota(jnp.int32, (tok, tok), 1)
            line = lax.broadcasted_iota(jnp.int32, (tok, tok), 0)
            seen = (across <= line) & (across.astype(F32) < length)
            bias = jnp.where(seen, 0.0, NEG).astype(F32)
            bias = jnp.concatenate([bias] * stack, axis=0)
            blocks.append((sk_ref[:, pl.ds(start, HD)], sv_ref[:, pl.ds(start, HD)], bias))
        for rows, ref in zip(rows_of, packs):
            lines = max(1, rows // width)
            groups = [ref[2 * rows + n : 2 * rows + n + 1, : rows // lines] for n in range(lines)]
            groups = groups[0] if lines == 1 else jnp.concatenate(groups, axis=1)
            groups = groups.astype(F32)
            bias = jnp.where(groups < jnp.broadcast_to(shots, groups.shape), 0.0, NEG).astype(F32)
            blocks.append((ref[0:rows, col], ref[rows : 2 * rows, col], bias))
        blocks = [(k, jnp.concatenate([v, jnp.ones_like(v)], axis=1), b) for k, v, b in blocks]

        def group(base):
            ats = [slice((base + i) * HD, (base + i + 1) * HD) for i in range(stack)]
            q = jnp.concatenate([q_ref[:, at] for at in ats], axis=0)
            scores = [
                dot(q, k, (((1,), (1,)), ((), ()))) * SCORE_SCALE + bias for k, _, bias in blocks
            ]
            peak = None
            for s in scores:
                for j in range(0, s.shape[1], 128):
                    part = s[:, j : j + 128]
                    peak = part if peak is None else jnp.maximum(peak, part)
            peak = jnp.max(peak, axis=1, keepdims=True)
            update = None
            for s, (_, v, _) in zip(scores, blocks):
                term = dot(jnp.exp2(s - peak).astype(BF), v)
                update = term if update is None else update + term
            for i, at in enumerate(ats):
                r = slice(i * tok, (i + 1) * tok)
                top, total = update[r, :HD], update[r, HD:]
                ctx_ref[:, at] = (top / total).astype(BF)
                level = jnp.broadcast_to(peak[r], (tok, HD)) + jnp.log2(total)
                lse_ref[...] = jnp.where(lane == base + i, level, lse_ref[...])

        for i in range(0, per_kv, stack):
            group(kv * per_kv + i)
        if not before and not last:
            continue
        levels = [lse_ref[...]] + [lse[...] for _, lse in before]
        bound = functools.reduce(jnp.maximum, levels)
        factors = [jnp.exp2(level - bound) for level in levels]
        total = functools.reduce(jnp.add, factors)
        shares = [factor / total for factor in factors[1:]]
        for h in range(kv * per_kv, (kv + 1) * per_kv):
            at = slice(h * HD, (h + 1) * HD)
            mine = ctx_ref[:, at].astype(F32)
            result = mine
            for (ctx, _), share in zip(before, shares):
                share = jnp.broadcast_to(share[:, h : h + 1], (tok, HD))
                result = result + (ctx[:, at].astype(F32) - mine) * share
            if last:
                store_ref[:, at] = jnp.where(live, result, 0.0).astype(BF)
            else:
                ctx_ref[:, at] = result.astype(BF)
        if last:
            at = slice(kv * per_kv * HD, (kv + 1) * per_kv * HD)
            stores.append(pltpu.make_async_copy(store_ref.at[:, at], out_ref.at[:, at], sem.at[kv]))
            stores[-1].start()
        elif kv == local_heads // per_kv - 1:
            lse_ref[...] = bound + jnp.log2(total)
    for store in stores:
        store.wait()


def attend(queries, facts, own, packs, before, last, per_kv, width, head_block, waits=()):
    tok, columns = queries.shape
    local_heads = columns // HD
    first = own is not None
    rows_of = tuple((p.shape[0] - GROUP_ROWS) // 2 for p in packs)
    cfg = (per_kv, width, head_block, rows_of, first, len(before), last, len(waits))
    operands = [facts, queries] + (list(own) if first else []) + list(packs)
    for pair in before:
        operands += list(pair)
    context = jax.ShapeDtypeStruct((tok, columns), BF)
    level = jax.ShapeDtypeStruct((tok, 128), F32)
    keys = sum(rows_of) + (tok if first else 0)
    scratch = []
    if last:
        scratch = [pltpu.VMEM((tok, columns), BF), pltpu.VMEM((tok, 128), F32), pltpu.VMEM((tok, columns), BF)]
        scratch.append(pltpu.SemaphoreType.DMA((max(1, local_heads // per_kv),)))
    return pl.pallas_call(
        functools.partial(attend_kernel, cfg),
        out_shape=context if last else [context, level],
        in_specs=[VMEM] * len(operands) + [ANY] * len(waits),
        out_specs=HBM if last else [VMEM, VMEM],
        scratch_shapes=scratch,
        compiler_params=params(ATT_MIB),
        cost_estimate=cost(8 * tok * local_heads * keys * HD, 4 * tok * columns),
        name="attend",
    )(*operands, *waits)


def earlier(tok):
    line = lax.broadcasted_iota(jnp.int32, (tok, tok), 0)
    lane = lax.broadcasted_iota(jnp.int32, (tok, tok), 1)
    return jnp.where(line < lane, 1.0, 0.0).astype(BF)


def routes(ids, expert_of, weights=None):
    shape = expert_of.shape
    taken = jnp.zeros(shape, F32)
    share = jnp.zeros(shape, F32)
    for k in range(TOP):
        match = jnp.broadcast_to(ids[k : k + 1, :], shape) == expert_of
        taken = jnp.where(match, 1.0, taken)
        if weights is not None:
            share = share + jnp.where(match, jnp.broadcast_to(weights[k : k + 1, :], shape), 0.0)
    slot = dot(taken.astype(BF), earlier(shape[1])).astype(jnp.int32)
    return taken, slot, share


def pack_kernel(width, head_block, k_ref, v_ref, g_ref, out_ref, groups_ref, held_ref, sem):
    rows = k_ref.shape[0]
    first = pl.multiple_of(head_block(lax.axis_index("tp")) * width, 128)
    copies = [pltpu.make_async_copy(g_ref, groups_ref, sem.at[2])]
    for n, ref in enumerate((k_ref, v_ref)):
        place = held_ref.at[n * rows : (n + 1) * rows, :]
        copies.append(pltpu.make_async_copy(ref.at[:, pl.ds(first, width)], place, sem.at[n]))
    for copy in copies:
        copy.start()
    copies[0].wait()
    groups = groups_ref[...].astype(F32)
    pad = jnp.full((GROUP_ROWS - groups.shape[0], groups.shape[1]), 0.0, F32)
    groups = jnp.concatenate([groups, pad], axis=0)
    if groups.shape[1] < width:
        filler = jnp.zeros((GROUP_ROWS, width - groups.shape[1]), F32)
        groups = jnp.concatenate([groups, filler], axis=1)
    held_ref[2 * rows :, :] = groups.astype(BF)
    copies[1].wait()
    copies[2].wait()
    store = pltpu.make_async_copy(held_ref, out_ref, sem.at[3])
    store.start()
    store.wait()


def make_pack(keys, values, groups, width, head_block):
    rows = keys.shape[0]
    lines = max(1, rows // width)
    shape = (2 * rows + GROUP_ROWS, width)
    return pl.pallas_call(
        functools.partial(pack_kernel, width, head_block),
        out_shape=jax.ShapeDtypeStruct(shape, BF),
        in_specs=[HBM] * 3,
        out_specs=HBM,
        scratch_shapes=[
            pltpu.VMEM((lines, rows // lines), jnp.int32),
            pltpu.VMEM(shape, BF),
            pltpu.SemaphoreType.DMA((4,)),
        ],
        compiler_params=pltpu.CompilerParams(vmem_limit_bytes=VMEM_ALL),
        cost_estimate=cost(0, 4 * rows * width * 4),
        name="pack",
    )(keys, values, groups.reshape(lines, rows // lines))


def target(me, n, size):
    return me ^ n if size & (size - 1) == 0 else lax.rem(me + n, size)


def select_kernel(cfg, place_ref, ids_ref, *refs):
    experts, parts = cfg
    hidden, outs = refs[:parts], refs[parts + 1 : parts + 1 + experts]
    own_ref, held_ref, here_ref, sem = refs[parts + 1 + experts :]
    tok, model = hidden[0].shape
    half = model // parts
    me = lax.axis_index("pp")
    column = pl.multiple_of(me * half, 128)
    copies = [pltpu.make_async_copy(ids_ref, own_ref, sem.at[0])]
    copies.append(pltpu.make_async_copy(place_ref, here_ref, sem.at[1 + parts]))
    for n in range(parts):
        source = hidden[n].at[:, pl.ds(column, half)]
        rows = held_ref.at[n * tok : (n + 1) * tok, :]
        copies.append(pltpu.make_async_copy(source, rows, sem.at[1 + n]))
    for copy in copies:
        copy.start()
    copies[0].wait()
    copies[1].wait()
    per = parts * CAP
    lines = experts * per
    row = lax.broadcasted_iota(jnp.int32, (lines, tok), 0)
    expert = target(here_ref[0], row // per, experts)
    picks = []
    for n in range(parts):
        block = lax.rem(me + parts - n, parts)
        ids = own_ref[:, pl.ds(pl.multiple_of(block * tok, tok), tok)]
        taken, slot, _ = routes(ids, expert)
        place = row % per
        chosen = (taken > 0.0) & (slot == place % CAP) & (place // CAP == block)
        picks.append(jnp.where(chosen, 1.0, 0.0))
    pick = jnp.concatenate(picks, axis=1)
    for copy in copies[2:]:
        copy.wait()
    for e in range(experts):
        outs[e][...] = dot(pick[e * per : (e + 1) * per, :].astype(BF), held_ref[...]).astype(BF)


def select(place, ids, hidden, experts, parts, wait):
    tok, model = hidden[0].shape
    half = model // parts
    return pl.pallas_call(
        functools.partial(select_kernel, (experts, parts)),
        out_shape=[jax.ShapeDtypeStruct((parts * CAP, half), BF)] * experts,
        in_specs=[HBM] * (2 + parts) + [ANY],
        out_specs=[VMEM] * experts,
        scratch_shapes=[
            pltpu.VMEM(ids.shape, jnp.int32),
            pltpu.VMEM((parts * tok, half), BF),
            pltpu.SMEM((1,), jnp.int32),
            pltpu.SemaphoreType.DMA((2 + parts,)),
        ],
        compiler_params=params(16),
        cost_estimate=cost(1e10, 2 * tok * model),
        name="select",
    )(place, ids, *hidden, wait)


def mark_kernel(*refs):
    refs[-1][...] = jnp.zeros_like(refs[-1])


def mark(flops, *waits):
    return pl.pallas_call(
        mark_kernel,
        out_shape=jax.ShapeDtypeStruct((8, 128), F32),
        in_specs=[ANY] * len(waits),
        out_specs=VMEM,
        compiler_params=params(1),
        cost_estimate=cost(flops, 4096),
        name="mark",
    )(*waits)


def gateup_kernel(pieces, waits, gate_ref, up_ref, *refs):
    out_ref = refs[pieces + waits]
    units = gate_ref.shape[2]
    x = jnp.concatenate([r[...].astype(F32) for r in refs[:pieces]], axis=0).astype(BF)
    for n, w_ref in enumerate((gate_ref, up_ref)):
        out_ref[:, n * units : (n + 1) * units] = dot(x, w_ref[0]).astype(BF)


def gateup(pieces, gate_proj, up_proj, waits=()):
    _, model, units = gate_proj.shape
    rows = sum(p.shape[0] for p in pieces)
    return pl.pallas_call(
        functools.partial(gateup_kernel, len(pieces), len(waits)),
        out_shape=jax.ShapeDtypeStruct((rows, 2 * units), BF),
        in_specs=[VMEM] * (2 + len(pieces)) + [ANY] * len(waits),
        out_specs=VMEM,
        compiler_params=params(16),
        cost_estimate=cost(4 * rows * model * units, 4 * model * units),
        name="gateup",
    )(gate_proj, up_proj, *pieces, *waits)


def down_kernel(splits, waits, mine_ref, other_ref, down_ref, *outs):
    outs = outs[waits:]
    units = mine_ref.shape[1] // 2
    total = mine_ref[...].astype(F32)
    for n in range(other_ref.shape[0]):
        total = total + other_ref[n].astype(F32)
    gate, up = total[:, :units], total[:, units:]
    active = (gate / (1.0 + jnp.exp(-gate)) * up).astype(BF)
    width = down_ref.shape[2] // splits
    me = lax.axis_index("tp")
    for n in range(splits):
        at = pl.ds(pl.multiple_of(target(me, n, splits) * width, 128), width)
        outs[n][...] = dot(active, down_ref[0, :, at]).astype(outs[n].dtype)


def down(mine, other, down_proj, splits, waits=()):
    rows = mine.shape[0]
    _, units, model = down_proj.shape
    shapes = [jax.ShapeDtypeStruct((rows, model // splits), F32 if n == 0 else BF) for n in range(splits)]
    return pl.pallas_call(
        functools.partial(down_kernel, splits, len(waits)),
        out_shape=shapes,
        in_specs=[VMEM] * 3 + [ANY] * len(waits),
        out_specs=[VMEM] * splits,
        compiler_params=params(16),
        cost_estimate=cost(2 * rows * model * units, 2 * model * units),
        name="down",
    )(mine, other, down_proj, *waits)


def join_kernel(experts, count, waits, *refs):
    parts, outs = refs[:count], refs[count + waits :]
    per = parts[0].shape[0] // experts
    for n in range(experts):
        at = slice(n * per, (n + 1) * per)
        total = parts[0][at, :]
        for p in parts[1:]:
            total = total + p[at, :].astype(F32)
        outs[n][...] = total.astype(BF)


def join(parts, experts, waits=()):
    rows, width = parts[0].shape
    return pl.pallas_call(
        functools.partial(join_kernel, experts, len(parts), len(waits)),
        out_shape=[jax.ShapeDtypeStruct((rows // experts, width), BF)] * experts,
        in_specs=[VMEM] * len(parts) + [ANY] * len(waits),
        out_specs=[VMEM] * experts,
        compiler_params=params(8),
        cost_estimate=cost(rows * width, 8 * rows * width),
        name="join",
    )(*parts, *waits)


def table_kernel(experts, parts, waits, place_ref, ids_ref, weight_ref, *refs):
    high_ref, low_ref, here_ref, sem = refs[waits:]
    copy = pltpu.make_async_copy(place_ref, here_ref, sem)
    copy.start()
    copy.wait()
    per = parts * CAP
    tok = ids_ref.shape[1] // parts
    row = lax.broadcasted_iota(jnp.int32, (experts * per, tok), 0)
    expert = target(here_ref[0], row // per, experts)
    place = row % per
    for p in range(parts):
        at = slice(p * tok, (p + 1) * tok)
        _, slot, share = routes(ids_ref[:, at], expert, weight_ref[:, at])
        chosen = (slot == place % CAP) & (place // CAP == p)
        table = jnp.where(chosen, share, 0.0)
        high = table.astype(BF)
        high_ref[:, at] = high
        low_ref[:, at] = (table - high.astype(F32)).astype(BF)


def make_table(place, ids, weights, experts, parts, waits=()):
    shape = jax.ShapeDtypeStruct((experts * parts * CAP, ids.shape[1]), BF)
    return pl.pallas_call(
        functools.partial(table_kernel, experts, parts, len(waits)),
        out_shape=[shape] * 2,
        in_specs=[HBM] + [VMEM] * 2 + [ANY] * len(waits),
        out_specs=[VMEM] * 2,
        scratch_shapes=[pltpu.SMEM((1,), jnp.int32), pltpu.SemaphoreType.DMA],
        compiler_params=params(8),
        cost_estimate=cost(1e6, 1e6),
        name="table",
    )(place, ids, weights, *waits)


def combine_kernel(high_ref, low_ref, *refs):
    backs, out_ref = refs[:-1], refs[-1]
    back = jnp.concatenate([b[...].astype(F32) for b in backs], axis=0).astype(BF)
    tn = (((0,), (0,)), ((), ()))
    out_ref[...] = (dot(high_ref[...], back, tn) + dot(low_ref[...], back, tn)).astype(BF)


def combine(high, low, backs):
    tokens = high.shape[1]
    width = backs[0].shape[1]
    return pl.pallas_call(
        combine_kernel,
        out_shape=jax.ShapeDtypeStruct((tokens, width), BF),
        in_specs=[VMEM] * (2 + len(backs)),
        out_specs=VMEM,
        compiler_params=params(16),
        cost_estimate=cost(4 * high.size * width, 4 * high.size + 2 * tokens * width),
        name="combine",
    )(high, low, *backs)


def swaps(size, k):
    return [(i, i ^ k) for i in range(size)]


def sends(size, n):
    if size & (size - 1) == 0:
        return swaps(size, n)
    return [(i, (i + n) % size) for i in range(size)]


def others(a, axis, size):
    return [lax.ppermute(a, axis, [(i, (i + k) % size) for i in range(size)]) for k in range(1, size)]


def layer(
    queries,
    suffix_keys,
    suffix_values,
    prefix_keys,
    prefix_values,
    prefix_groups,
    shot_counts,
    lengths,
    hidden,
    expert_ids,
    gate_weights,
    gate_proj,
    up_proj,
    down_proj,
):
    ep, tp, pp = lax.axis_size("ep"), lax.axis_size("tp"), lax.axis_size("pp")
    local_heads = queries.shape[1] // HD
    head_group = HEADS // KVH
    kv_heads = max(1, local_heads // head_group)
    per_kv = min(local_heads, head_group)
    width = kv_heads * HD

    def head_block(tp_index):
        return (tp_index * local_heads // head_group) // kv_heads

    rows = prefix_keys.shape[0]
    ids, shares = expert_ids.T, gate_weights.T
    place = lax.axis_index("ep").reshape(1)
    fixed = dict(per_kv=per_kv, width=width, head_block=head_block)
    own = (suffix_keys, suffix_values)

    features = [hidden] + others(hidden, "pp", pp)
    pack = make_pack(prefix_keys, prefix_values, prefix_groups, width, head_block)
    line = lax.broadcasted_iota(jnp.int32, (16, 128), 0)
    facts = jnp.where(line < 8, shot_counts[:, None], lengths[:, None]).astype(F32)
    basic = (queries, facts)
    packed = mark(1e10)
    outgoing = select(place, ids, features, ep, pp, packed)
    arrived = [outgoing[0]]
    for n in reversed(range(1, ep)):
        arrived.insert(1, lax.ppermute(outgoing[n], "ep", sends(ep, n)))

    ringed = ep & (ep - 1) == 0 and rows % 128 == 0
    if ringed:
        held = [pack]
        stride = ep // 2
        while stride:
            first, *rest = held
            moved = [lax.ppermute(first, "ep", swaps(ep, stride))]
            moved += [lax.ppermute(b, "ep", swaps(ep, stride)) for b in rest]
            held += moved
            stride //= 2
        order = [0, ep // 2] + [n for n in range(1, ep) if n != ep // 2]
        chips = []
        for n in order[:ep]:
            chips.append([held[n]] + others(held[n], "pp", pp))
    else:
        every = lax.all_gather(pack, ("ep", "pp"), axis=0)
        step = max(1, 256 // rows)
        keys = every[:, :rows].reshape(-1, step * rows, width)
        values = every[:, rows : 2 * rows].reshape(-1, step * rows, width)
        lines = max(1, rows // width)
        groups = every[:, 2 * rows : 2 * rows + lines, : rows // lines].reshape(-1, step * rows // width, width)
        groups = jnp.pad(groups, ((0, 0), (0, GROUP_ROWS - groups.shape[1]), (0, 0)))
        joined = jnp.concatenate([keys, values, groups], axis=1)
        chips = [[joined[n] for n in range(joined.shape[0])]]

    partial = []

    def attend_chip(n, waits):
        last = n == len(chips) - 1
        before = partial if last or n == 1 else []
        result = attend(*basic, own if n == 0 else None, chips[n], before, last, waits=waits, **fixed)
        if not last:
            partial[:] = [result] if n == 1 else partial + [result]
        return (result if last else result[1],)

    turn = iter(range(len(chips)))
    wait = attend_chip(next(turn), (outgoing[0],)) if len(chips) > 1 else (outgoing[0],)
    wait = attend_chip(next(turn), wait) if len(chips) > 2 else wait

    mine = gateup(arrived, gate_proj, up_proj, wait)
    other = others(mine, "pp", pp)
    other = jnp.stack(other) if pp > 2 else other[0][None]
    high, low = make_table(place, ids, shares, ep, pp, (mine,))
    parts = down(mine, other, down_proj, tp, (high,))
    received = []
    for n in range(1, tp):
        received.append(lax.ppermute(parts[n], "tp", sends(tp, n)))
    wait = (mark(1e6, parts[0]),)
    wait = attend_chip(next(turn), wait) if len(chips) > 3 else wait
    done = join([parts[0]] + received, ep, wait)
    backs = [done[0]]
    for n in reversed(range(1, ep)):
        backs.insert(1, lax.ppermute(done[n], "ep", [(t, f) for f, t in sends(ep, n)]))
    wait = (mark(1e6, done[0]),)
    for n in turn:
        wait = attend_chip(n, wait)
    (context,) = wait
    moe_out = combine(high, low, backs)
    return (context, moe_out)


def solution(mesh):
    placed = (
        P(("grp", "ep", "pp"), "tp"),
        P(("grp", "ep", "pp"), None),
        P(("grp", "ep", "pp"), None),
        P(("grp", "ep", "pp"), None),
        P(("grp", "ep", "pp"), None),
        P(("grp", "ep", "pp")),
        P(("grp", "ep", "pp")),
        P(("grp", "ep", "pp")),
        P(("grp", "ep", "pp"), None),
        P(("grp", "ep"), None),
        P(("grp", "ep"), None),
        P("ep", "pp", "tp"),
        P("ep", "pp", "tp"),
        P("ep", "tp", "pp"),
    )
    return jax.shard_map(
        layer,
        mesh=mesh,
        in_specs=placed,
        out_specs=(P(("grp", "ep", "pp"), "tp"), P(("grp", "ep"), ("pp", "tp"))),
        check_vma=False,
    )
```
